32 devices in a mesh: groups: 2 (over x), inner: 16 (over z, y, core).
Axes of the slice: x: 2, y: 2, z: 4, core: 2. Of those that a mesh axis runs over, the one named last changes fastest.
Arguments:
- hidden_rows: bfloat16 [2048, 2048], P(('groups', 'inner')), parts along dimension 0, may hold values from -6 to 6
- token_embed: bfloat16 [2048, 2048], P(('groups', 'inner')), parts along dimension 0, may hold values from -6 to 6
- first_routes: int32 [2048, 8], P(('groups', 'inner')), parts along dimension 0, may hold values from 0 to 15, all different within a row; in each aligned block of 64 rows (0 to 63, 64 to 127, ...) at most 48 rows name the same one
- first_gates: float32 [2048, 8], P(('groups', 'inner')), parts along dimension 0, may hold values from 0.2 to 0.6
- first_gate_up: bfloat16 [16, 2048, 1024], P('inner'), may hold values from -0.125 to 0.125
- first_down: bfloat16 [16, 512, 2048], P('inner'), may hold values from -0.25 to 0.25
- second_routes: int32 [2048, 8], P(('groups', 'inner')), parts along dimension 0, may hold values from 0 to 15, all different within a row; in each aligned block of 64 rows (0 to 63, 64 to 127, ...) at most 48 rows name the same one
- second_gates: float32 [2048, 8], P(('groups', 'inner')), parts along dimension 0, may hold values from 0.2 to 0.6
- second_gate_up: bfloat16 [16, 2048, 1024], P('inner'), may hold values from -0.125 to 0.125
- second_down: bfloat16 [16, 512, 2048], P('inner'), may hold values from -0.25 to 0.25
- hidden_gain: float32 [2048], replicated, may hold values from 0.25 to 1.75
- embed_gain: float32 [2048], replicated, may hold values from 0.25 to 1.75
- merge_weight: bfloat16 [4096, 2048], P('inner'), may hold values from -0.09375 to 0.09375
Outputs:
- final_rows: bfloat16 [2048, 2048], P(('groups', 'inner')), parts along dimension 0
The draws below stay inside these ranges and needn't reach their ends.
There are 2 independent parts, one for each index of `groups`. The reference program is written for one: setup_inputs(seed, part) draws one part's arguments, and reference() takes and returns one part's arrays. A program takes and returns all parts, laid end to end along the dimension named above; an argument that names none is the same for every part. Nothing has to cross between parts.
Inputs may be any that keep to these rules, and one draw needn't show every extreme that they name: `first_routes`: among the 64 tokens of one block, no expert is named more than 48 times, and in every draw some expert is named exactly 48 times in some block. `second_routes`: among the 64 tokens of one block, no expert is named more than 48 times, and in every draw some expert is named exactly 48 times in some block.
All inputs are finite; a program needn't handle non-finite values.
Results may differ from the reference program's by a relative error of at most 0.01.
Values may be sent and summed in bfloat16 or wider, within the bound.
A program may use at most 128 MiB of HBM per device.

```python
import math
import jax
import jax.numpy as jnp
import numpy as np
from jax import lax

D = 2048
FFW = 512
TOP = 8
TOK_DEV = 64
EXPERTS = 16
TOKENS = 1024
CAP = 48
N_INNER = 16


def block_scale(key, extent, pieces, low, top_value):
    def one(axis_at, blocks):
        steps = jax.random.uniform(jax.random.fold_in(jax.random.fold_in(key, 6), axis_at), (blocks,), jnp.float32, low / len(pieces), top_value / len(pieces))
        return jnp.repeat(jnp.exp(steps), extent[axis_at] // blocks).reshape((-1,) + (1,) * (len(extent) - axis_at - 1))

    loudness = one(*pieces[0])
    for cut in pieces[1:]:
        loudness = loudness * one(*cut)
    return loudness


def deal_out(rng, own, number, rows, count, top, most, skew):
    order = jax.random.permutation(rng, count)
    heavy_load, usual = shares(count, rows * top, most, skew, True), shares(count, rows * top, most, skew, False)
    places = jnp.arange(count)

    def named(tallies, turn):
        used = int((tallies > 0).sum())
        fixed = max(1, used // 4)
        passed = fixed + (places - fixed + turn * (used - fixed)) % max(1, count - fixed)
        return jnp.zeros((count,), jnp.int32).at[order[jnp.where(places < fixed, places, passed)]].set(jnp.asarray(tallies, jnp.int32))

    tallies = jnp.where(number % 4 == 0, named(heavy_load, number // 4), named(usual, number - number // 4 - 1))
    mixed = jax.random.permutation(jax.random.fold_in(own, 3), count)
    giver, receiver = mixed[0:count // 2 * 2:2], mixed[1:count // 2 * 2:2]
    slack = jnp.minimum(tallies[giver] - 1, most - tallies[receiver]) // 2
    slack = jnp.where((giver == order[0]) | (receiver == order[0]) | (tallies[receiver] == 0), 0, jnp.maximum(slack, 0))
    passed = jax.random.randint(jax.random.fold_in(own, 4), (count // 2,), 0, 1 << 20) % (slack + 1)
    tallies = tallies.at[giver].add(-passed).at[receiver].add(passed)
    labels = jnp.searchsorted(jnp.cumsum(tallies), jnp.arange(rows * top), side="right").astype(jnp.int32)
    listing = labels.reshape(top, rows).T
    listing = listing[jax.random.permutation(jax.random.fold_in(own, 1), rows)]
    turn = jax.random.randint(jax.random.fold_in(own, 2), (rows, 1), 0, top)
    return jnp.take_along_axis(listing, (jnp.arange(top)[None, :] + turn) % top, axis=1)


def shares(amount, total, limit, slope, full):
    weights = [(1 << 20) // math.isqrt(rank ** slope) + 1 for rank in range(1, amount + 1)]
    largest = limit if full else min(limit, max(-(-total // amount), total * weights[0] // sum(weights)))
    least = 1 if total - largest >= amount - 1 else 0
    holding, spare = [largest] + [least] * (amount - 1), total - largest - least * (amount - 1)
    while spare > 0:
        candidates = [i for i in range(1, amount) if holding[i] < largest] or [i for i in range(1, amount) if holding[i] < limit]
        whole, budget = sum([weights[i] for i in candidates]), spare
        for i in candidates:
            more = min(limit - holding[i], max(1, budget * weights[i] // whole), spare)
            holding[i] = holding[i] + more
            spare = spare - more
    return np.array(holding)


def bell_draw(own_key, extent, spread, reach, cuts=(), held_as=jnp.bfloat16):
    values = jax.random.normal(own_key, extent, jnp.float32) * spread
    if len(cuts) > 0:
        values = block_scale(own_key, extent, cuts, -0.22, 0.18) * values
    return jnp.clip(values, min=-reach, max=reach).astype(held_as)


def setup_inputs(seed: int = 0, part: int = 0) -> dict:
    key_of = jax.random.split(jax.random.key(seed), 14)
    part_splits = jax.random.split(jax.random.fold_in(key_of[13], part), 14)
    hidden_rows = bell_draw(part_splits[0], (TOKENS, D), 1.0, 6.0, ((0, 16),))
    token_embed = bell_draw(part_splits[1], (TOKENS, D), 1.0, 6.0, ((0, 16),))
    first_routes_keys = jax.random.split(jax.random.fold_in(part_splits[2], 1), TOKENS // TOK_DEV)
    first_routes_turns = jax.random.permutation(jax.random.fold_in(part_splits[2], 3), TOKENS // TOK_DEV)
    first_routes = jax.vmap(lambda own, number: deal_out(jax.random.fold_in(part_splits[2], 2), own, number, TOK_DEV, EXPERTS, TOP, CAP, 2))(first_routes_keys, first_routes_turns).reshape((TOKENS, TOP))
    first_gates = jnp.clip(0.2 + 0.400000021 * jax.random.uniform(part_splits[3], (TOKENS, TOP), jnp.float32) ** block_scale(part_splits[3], (TOKENS, TOP), ((0, 16),), -0.2, 0.2), 0.2, 0.6)
    first_gate_up = bell_draw(key_of[4], (EXPERTS, D, 2 * FFW), D ** -0.5, 0.125, ((0, 16),))
    first_down = bell_draw(key_of[5], (EXPERTS, FFW, D), FFW ** -0.5, 0.25, ((0, 16),))
    second_routes_keys = jax.random.split(jax.random.fold_in(part_splits[6], 1), TOKENS // TOK_DEV)
    second_routes_turns = jax.random.permutation(jax.random.fold_in(part_splits[6], 3), TOKENS // TOK_DEV)
    second_routes = jax.vmap(lambda own, number: deal_out(jax.random.fold_in(part_splits[6], 2), own, number, TOK_DEV, EXPERTS, TOP, CAP, 1))(second_routes_keys, second_routes_turns).reshape((TOKENS, TOP))
    second_gates = jnp.clip(0.2 + 0.400000021 * jax.random.uniform(part_splits[7], (TOKENS, TOP), jnp.float32) ** block_scale(part_splits[7], (TOKENS, TOP), ((0, 16),), -0.2, 0.2), 0.2, 0.6)
    second_gate_up = bell_draw(key_of[8], (EXPERTS, D, 2 * FFW), D ** -0.5, 0.125, ((0, 16),))
    second_down = bell_draw(key_of[9], (EXPERTS, FFW, D), FFW ** -0.5, 0.25, ((0, 16),))
    hidden_gain = jnp.clip(1.0 + 0.15 * jax.random.normal(key_of[10], (D,), jnp.float32), 0.25, 1.75)
    embed_gain = jnp.clip(1.0 + 0.15 * jax.random.normal(key_of[11], (D,), jnp.float32), 0.25, 1.75)
    merge_weight = bell_draw(key_of[12], (2 * D, D), (2 * D) ** -0.5, 0.09375, ((0, 16),))
    return dict(hidden_rows=hidden_rows, token_embed=token_embed, first_routes=first_routes, first_gates=first_gates, first_gate_up=first_gate_up, first_down=first_down, second_routes=second_routes, second_gates=second_gates, second_gate_up=second_gate_up, second_down=second_down, hidden_gain=hidden_gain, embed_gain=embed_gain, merge_weight=merge_weight)


EPSILON = 1e-06

def expert_apply(slot_rows, expert_gu, expert_down):
    inner_width = expert_down.shape[0]
    projected = jnp.dot(slot_rows, expert_gu, preferred_element_type=jnp.float32)
    inner = (jax.nn.silu(projected[:, :inner_width]) * projected[:, inner_width:]).astype(jnp.bfloat16)
    return jnp.dot(inner, expert_down, preferred_element_type=jnp.float32).astype(jnp.bfloat16)

def rms_scale(values, gain_vec):
    widened = values.astype(jnp.float32)
    inverse_rms = lax.rsqrt(lax.optimization_barrier(jnp.mean(widened * widened, axis=-1, keepdims=True)) + EPSILON)
    return (widened * inverse_rms * gain_vec.astype(jnp.float32)).astype(jnp.bfloat16)

def routed_reference(inputs, routes, weights_in, gate_up, down_proj):
    tokens_all, feature_dim = inputs.shape
    top_count = routes.shape[1]
    experts = gate_up.shape[0]
    blocks = N_INNER
    per_block = tokens_all // blocks
    capacity = max(2, 3 * per_block * top_count // (2 * experts))
    grouped = routes.reshape(blocks, per_block * top_count)
    onehot = (grouped[:, :, None] == jnp.arange(experts, dtype=jnp.int32)[None, None, :]).astype(jnp.int32)
    ranking = lax.optimization_barrier(jnp.sum(onehot * (jnp.cumsum(onehot, axis=1) - 1), axis=2))
    source = jnp.arange(blocks, dtype=jnp.int32)[:, None] * capacity
    position = (grouped * (blocks * capacity) + source + ranking).reshape(-1).astype(jnp.int32)
    repeated = jnp.repeat(inputs, top_count, axis=0)
    buffer_rows = jnp.zeros((experts * blocks * capacity, feature_dim), jnp.bfloat16).at[position].set(repeated)

    def one_expert(operands):
        slot_rows, expert_gu, expert_down = operands
        return expert_apply(slot_rows, expert_gu, expert_down)
    outputs = lax.map(one_expert, (buffer_rows.reshape(experts, blocks * capacity, feature_dim), gate_up, down_proj))
    picked = outputs.reshape(-1, feature_dim)[position].reshape(tokens_all, top_count, feature_dim)
    return lax.optimization_barrier(jnp.sum(picked.astype(jnp.float32) * weights_in.astype(jnp.float32)[:, :, None], axis=1))

def reference(hidden_rows, token_embed, first_routes, first_gates, first_gate_up, first_down, second_routes, second_gates, second_gate_up, second_down, hidden_gain, embed_gain, merge_weight):
    first_moe = routed_reference(hidden_rows, first_routes, first_gates, first_gate_up, first_down)
    after_first = (hidden_rows.astype(jnp.float32) + first_moe).astype(jnp.bfloat16)
    merged_in = jnp.concatenate([rms_scale(after_first, hidden_gain), rms_scale(token_embed, embed_gain)], axis=1)
    merged = jnp.dot(merged_in, merge_weight, preferred_element_type=jnp.float32)
    after_merge = (after_first.astype(jnp.float32) + jax.nn.silu(merged)).astype(jnp.bfloat16)
    second_moe = routed_reference(after_merge, second_routes, second_gates, second_gate_up, second_down)
    return (after_merge.astype(jnp.float32) + second_moe).astype(jnp.bfloat16)
```

```python
import jax
import jax.numpy as jnp
from jax import lax
from jax.sharding import PartitionSpec as P

EPSILON = 1e-06


def rms_scale(values, gain_vec):
    widened = values.astype(jnp.float32)
    inverse_rms = lax.rsqrt(jnp.mean(widened * widened, axis=-1, keepdims=True) + EPSILON)
    return (widened * inverse_rms * gain_vec).astype(jnp.bfloat16)


def dense_gates(routes, gates, experts):
    hit = routes[:, :, None] == jnp.arange(experts, dtype=jnp.int32)[None, None, :]
    return jnp.sum(jnp.where(hit, gates[:, :, None], 0.0), axis=1)


def dense_layer(rows, gate_column, gate_up, down):
    everyone = lax.all_gather(rows, "inner", axis=0, tiled=True)
    width = down.shape[0]
    projected = jnp.dot(everyone, gate_up, preferred_element_type=jnp.float32)
    inner = (jax.nn.silu(projected[:, :width]) * projected[:, width:]).astype(jnp.bfloat16)
    out = jnp.dot(inner, down, preferred_element_type=jnp.float32)
    share = jnp.where(gate_column > 0, out * gate_column, 0.0).astype(jnp.bfloat16)
    return lax.psum_scatter(share, "inner", scatter_dimension=0, tiled=True).astype(jnp.float32)


def local(
    hidden_rows,
    token_embed,
    first_routes,
    first_gates,
    first_gate_up,
    first_down,
    second_routes,
    second_gates,
    second_gate_up,
    second_down,
    hidden_gain,
    embed_gain,
    merge_weight,
):
    experts = lax.axis_size("inner")
    me = lax.axis_index("inner")
    both = jnp.concatenate(
        [
            dense_gates(first_routes, first_gates, experts),
            dense_gates(second_routes, second_gates, experts),
        ],
        axis=1,
    )
    both = lax.all_gather(both, "inner", axis=0, tiled=True)
    first_column = lax.dynamic_slice_in_dim(both, me, 1, axis=1)
    second_column = lax.dynamic_slice_in_dim(both, me + experts, 1, axis=1)

    first_moe = dense_layer(hidden_rows, first_column, first_gate_up[0], first_down[0])
    after_first = (hidden_rows.astype(jnp.float32) + first_moe).astype(jnp.bfloat16)
    merged_in = jnp.concatenate(
        [rms_scale(after_first, hidden_gain), rms_scale(token_embed, embed_gain)], axis=1
    )
    columns = lax.all_to_all(merged_in, "inner", split_axis=1, concat_axis=0, tiled=True)
    partial = jnp.dot(columns, merge_weight, preferred_element_type=jnp.float32)
    merged = lax.psum_scatter(
        partial.astype(jnp.bfloat16), "inner", scatter_dimension=0, tiled=True
    ).astype(jnp.float32)
    after_merge = (after_first.astype(jnp.float32) + jax.nn.silu(merged)).astype(jnp.bfloat16)
    second_moe = dense_layer(after_merge, second_column, second_gate_up[0], second_down[0])
    return (after_merge.astype(jnp.float32) + second_moe).astype(jnp.bfloat16)


def solution(mesh):
    rows = P(("groups", "inner"), None)
    return jax.shard_map(
        local,
        mesh=mesh,
        in_specs=(
            rows, rows, rows, rows,
            P("inner", None, None),
            P("inner", None, None),
            rows, rows,
            P("inner", None, None),
            P("inner", None, None),
            P(),
            P(),
            P("inner", None),
        ),
        out_specs=rows,
        check_vma=False,
    )
```

```python
import functools

import jax
import jax.numpy as jnp
from jax import lax
from jax.experimental import pallas as pl
from jax.experimental.pallas import tpu as pltpu
from jax.sharding import PartitionSpec as P

EPSILON = 1e-06
LANES = 128
VMEM_LIMIT = 60 * 1024 * 1024


class Ring:
    def __init__(self, devices, tok):
        self.devices, self.tok = devices, tok
        self.chips = devices // 2
        self.reach = self.chips // 2
        self.rise = self.chips // 2
        me = lax.axis_index("inner")
        chip = me // 2
        across = chip % 2
        along = chip // 2
        self.core = me % 2
        self.place = along * (1 - across) + (2 * self.rise - 1 - along) * across
        self.me = me

    def device(self, shift, other):
        place = (self.place + shift + self.chips) % self.chips
        across = place // self.rise
        along = place * (1 - across) + (2 * self.rise - 1 - place) * across
        core = self.core * (1 - other) + (1 - self.core) * other
        return (along * 2 + across) * 2 + core

    def row(self, way, distance, other):
        if distance == 0:
            return ((self.reach - 1) * 4 + 2 + other) * self.tok
        if distance == self.reach:
            return ((self.reach - 1) * 4 + other) * self.tok
        return ((distance - 1) * 4 + way * 2 + other) * self.tok

    def half(self, way, distance, other, k):
        part = self.tok // 2
        return pl.ds(self.row(way, distance, other) + k * part, part)

    def block(self, way, distance, other):
        return pl.ds(self.row(way, distance, other), self.tok)


def remote(src, dst, send, recv, device):
    return pltpu.make_async_remote_copy(
        src_ref=src, dst_ref=dst, send_sem=send, recv_sem=recv,
        device_id={"inner": device}, device_id_type=pl.DeviceIdType.MESH,
    )


def greet(devices):
    barrier = pltpu.get_barrier_semaphore()
    for device in devices:
        pl.semaphore_signal(
            barrier, inc=1, device_id={"inner": device}, device_id_type=pl.DeviceIdType.MESH
        )
    pl.semaphore_wait(barrier, len(devices))


def wide(values):
    return values.astype(jnp.float32)


def narrow(values):
    return values.astype(jnp.bfloat16)


class Reduce:
    def __init__(self, ring, share, paired, arrived, sems):
        self.ring, self.share, self.paired, self.arrived = ring, share, paired, arrived
        self.pair_send, self.pair_recv, self.send, self.recv = sems
        self.started = []

    def slots(self, distance):
        return ((0,) if distance in (0, self.ring.reach) else (0, 1))

    def pair_copy(self, way, distance):
        ring = self.ring
        slot = ring.reach * 2 if distance == 0 else (distance - 1) * 2 + way
        here = self.paired.at[pl.ds(slot * ring.tok, ring.tok)]
        return remote(
            self.share.at[ring.block(way, distance, 1)], here,
            self.pair_send.at[slot], self.pair_recv.at[slot], ring.device(0, 1),
        ), here

    def start_pair(self, distance):
        for way in self.slots(distance):
            copy, _ = self.pair_copy(way, distance)
            copy.start()
            self.started.append(copy)

    def finish_pair(self, distance):
        for way in self.slots(distance):
            copy, here = self.pair_copy(way, distance)
            copy.wait_recv()
            rows = self.ring.block(way, distance, 0)
            self.share[rows, :] = narrow(wide(self.share[rows, :]) + wide(here[...]))

    def hop(self, way, distance, k):
        ring = self.ring
        part = ring.tok // 2
        slot = (way * ring.reach + distance - 1) * 2 + k
        landing = self.arrived.at[pl.ds(slot * part, part)]
        return remote(
            self.share.at[ring.half(1 - way, distance, 0, k)], landing,
            self.send.at[slot], self.recv.at[slot], ring.device(1 - 2 * way, 0),
        ), landing

    def start_hop(self, way, distance, k):
        copy, _ = self.hop(way, distance, k)
        copy.start()
        self.started.append(copy)

    def step(self, way, distance, k):
        copy, landing = self.hop(way, distance + 1, k)
        copy.wait_recv()
        rows = self.ring.half(1 - way, distance, 0, k)
        self.share[rows, :] = narrow(wide(self.share[rows, :]) + wide(landing[...]))
        self.start_hop(way, distance, k)

    def early(self):
        reach = self.ring.reach
        if reach > 1:
            for way in (0, 1):
                self.start_hop(way, reach - 1, 1 - way)

    def late(self):
        reach = self.ring.reach
        for way in (0, 1):
            self.start_hop(way, reach, way)

    def run(self, base, out):
        reach = self.ring.reach
        for distance in range(reach - 1, 0, -1):
            for way in (0, 1):
                self.step(way, distance, way)
            if distance > 1:
                for way in (0, 1):
                    self.step(way, distance - 1, 1 - way)
        part = self.ring.tok // 2
        for k in (0, 1):
            total = wide(self.share[self.ring.half(0, 0, 0, k), :])
            for way in (0, 1):
                if k == way or reach > 1:
                    copy, landing = self.hop(way, 1, k)
                    copy.wait_recv()
                    total = total + wide(landing[...])
            rows = pl.ds(k * part, part)
            out[rows, :] = base(rows, total)
        for copy in self.started:
            copy.wait_send()


def reduce_scratch(devices, tok, width):
    chips = devices // 2
    reach = chips // 2
    return [
        pltpu.VMEM((devices * tok, width), jnp.bfloat16),
        pltpu.VMEM(((2 * reach + 1) * tok, width), jnp.bfloat16),
        pltpu.VMEM((2 * reach * tok, width), jnp.bfloat16),
        pltpu.SemaphoreType.DMA((2 * reach + 1,)),
        pltpu.SemaphoreType.DMA((2 * reach + 1,)),
        pltpu.SemaphoreType.DMA((4 * reach,)),
        pltpu.SemaphoreType.DMA((4 * reach,)),
    ]


def layer_kernel(
    devices, x_ref, gu_ref, down_ref, out_ref, everyone, gu, down, inner,
    share, paired, arrived, pair_send, pair_recv, hop_send, hop_recv,
    load_sem, send, recv, sib_send, sib_recv,
):
    tok = x_ref.shape[0]
    width = out_ref.shape[1]
    hidden = down.shape[0]
    ring = Ring(devices, tok)
    reach = ring.reach
    part = tok // 2
    loads = [
        pltpu.make_async_copy(gu_ref.at[0], gu, load_sem.at[0]),
        pltpu.make_async_copy(down_ref.at[0], down, load_sem.at[1]),
    ]
    for load in loads:
        load.start()
    greet([ring.device(1, 0), ring.device(-1, 0), ring.device(0, 1)])
    started = []

    def ring_copy(way, distance, k):
        slot = (way * reach + distance - 1) * 2 + k
        landing = everyone.at[ring.half(way, distance, 0, k)]
        source = (
            x_ref.at[pl.ds(k * part, part)]
            if distance == 1
            else everyone.at[ring.half(way, distance - 1, 0, k)]
        )
        return remote(source, landing, send.at[slot], recv.at[slot], ring.device(1 - 2 * way, 0))

    def sibling_copy(way, distance, k):
        slot = 4 * reach if distance == 0 else (way * reach + distance - 1) * 2 + k
        if distance == 0:
            source, landing = x_ref, everyone.at[ring.block(0, 0, 1)]
        else:
            source = everyone.at[ring.half(way, distance, 0, k)]
            landing = everyone.at[ring.half(way, distance, 1, k)]
        return remote(source, landing, sib_send.at[slot], sib_recv.at[slot], ring.device(0, 1))

    def begin(copy):
        copy.start()
        started.append(copy)

    reducing = Reduce(ring, share, paired, arrived, (pair_send, pair_recv, hop_send, hop_recv))

    def compute(distance):
        rows = pl.ds((distance - 1) * 4 * tok, 4 * tok)
        x = everyone.at[rows]
        step = min(256, hidden)

        @pl.loop(0, hidden // step)
        def _(j):
            left = pl.ds(pl.multiple_of(j * step, step), step)
            right = pl.ds(pl.multiple_of(hidden + j * step, step), step)
            g = jnp.dot(x[:, :width], gu[:, left], preferred_element_type=jnp.float32)
            u = jnp.dot(x[:, :width], gu[:, right], preferred_element_type=jnp.float32)
            inner[:, left] = narrow(jax.nn.silu(g) * u)

        pad = x.shape[1] - width
        lane = lax.broadcasted_iota(jnp.int32, (4 * tok, pad), 1)
        mine = (lane == ring.me) | (lane == ring.me + devices)
        gate = jnp.sum(jnp.where(mine, wide(x[:, width:]), 0.0), axis=1, keepdims=True)
        span = min(512, width)

        @pl.loop(0, width // span)
        def _(j):
            columns = pl.ds(pl.multiple_of(j * span, span), span)
            out = jnp.dot(inner[...], down[:, columns], preferred_element_type=jnp.float32)
            share[rows, columns] = narrow(out * gate)

    for way in (0, 1):
        begin(ring_copy(way, 1, way))
    for way in (0, 1):
        if reach > 1:
            begin(ring_copy(way, 1, 1 - way))
    begin(sibling_copy(0, 0, 0))
    everyone[ring.block(0, 0, 0), :] = x_ref[...]

    def arrivals(distance):
        for short in (0, 1):
            for way in (0, 1):
                k = way if short == 0 else 1 - way
                if short and distance == reach:
                    continue
                ring_copy(way, distance, k).wait_recv()
                if distance < reach and not (short and distance == reach - 1):
                    begin(ring_copy(way, distance + 1, k))
                begin(sibling_copy(way, distance, k))

    def sibling_arrivals(distance):
        for short in (0, 1):
            for way in (0, 1):
                k = way if short == 0 else 1 - way
                if short and distance == reach:
                    continue
                sibling_copy(way, distance, k).wait_recv()

    for distance in range(1, reach + 1):
        arrivals(distance)
        if distance == 1:
            for load in loads:
                load.wait()
        else:
            sibling_arrivals(distance - 1)
            compute(distance - 1)
            reducing.start_pair(distance - 1)
    for distance in range(1, reach):
        reducing.finish_pair(distance)
    reducing.early()
    sibling_arrivals(reach)
    sibling_copy(0, 0, 0).wait_recv()
    compute(reach)
    reducing.start_pair(reach)
    reducing.start_pair(0)
    reducing.finish_pair(reach)
    reducing.late()
    reducing.finish_pair(0)
    reducing.run(lambda rows, total: narrow(wide(x_ref[rows, :width]) + total), out_ref)
    for copy in started:
        copy.wait_send()


def routed_layer(devices, number, rows, routes, gates, gate_up, down):
    tok, width = rows.shape
    reach = devices // 4
    dense = dense_gates(routes, gates, devices)
    high = narrow(dense)
    low = narrow(dense - wide(high))
    pad = -(-2 * devices // LANES) * LANES - 2 * devices
    packed = jnp.concatenate([rows, high, low, jnp.zeros((tok, pad), jnp.bfloat16)], axis=1)
    hidden = down.shape[1]
    vmem = pl.BlockSpec(memory_space=pltpu.VMEM)
    return pl.pallas_call(
        functools.partial(layer_kernel, devices),
        out_shape=jax.ShapeDtypeStruct((tok, width), jnp.bfloat16),
        in_specs=[vmem, pl.BlockSpec(memory_space=pl.ANY), pl.BlockSpec(memory_space=pl.ANY)],
        out_specs=vmem,
        scratch_shapes=[
            pltpu.VMEM((devices * tok, packed.shape[1]), jnp.bfloat16),
            pltpu.VMEM(gate_up.shape[1:], jnp.bfloat16),
            pltpu.VMEM(down.shape[1:], jnp.bfloat16),
            pltpu.VMEM((4 * tok, hidden), jnp.bfloat16),
        ]
        + reduce_scratch(devices, tok, width)
        + [
            pltpu.SemaphoreType.DMA((2,)),
            pltpu.SemaphoreType.DMA((4 * reach,)),
            pltpu.SemaphoreType.DMA((4 * reach,)),
            pltpu.SemaphoreType.DMA((4 * reach + 1,)),
            pltpu.SemaphoreType.DMA((4 * reach + 1,)),
        ],
        compiler_params=pltpu.CompilerParams(
            collective_id=number, has_side_effects=True, vmem_limit_bytes=VMEM_LIMIT
        ),
    )(packed, gate_up, down)


def merge_kernel(
    devices, pieces_ref, rows_ref, weight_ref, out_ref, columns,
    share, paired, arrived, pair_send, pair_recv, hop_send, hop_recv, send, recv, own_sem,
):
    tok, width = rows_ref.shape
    ring = Ring(devices, tok)
    reach = ring.reach
    partners = [(0, 0, 1)]
    for distance in range(1, reach + 1):
        for other in (0, 1):
            partners.append((0, distance, other))
            if distance < reach:
                partners.append((1, distance, other))

    def shift(way, distance):
        return distance * (1 - 2 * way)

    own = pltpu.make_async_copy(
        pieces_ref.at[ring.me], columns.at[ring.block(0, 0, 0)], own_sem
    )
    own.start()
    greet([ring.device(shift(way, distance), other) for way, distance, other in partners])

    def piece(way, distance, other):
        target = ring.device(shift(way, distance), other)
        slot = ring.row(way, distance, other) // tok
        landing = columns.at[ring.block(way, distance, other)]
        return remote(pieces_ref.at[target], landing, send.at[slot], recv.at[slot], target)

    sent = [piece(*partner) for partner in reversed(partners)]
    for copy in sent:
        copy.start()
    own.wait()
    reducing = Reduce(ring, share, paired, arrived, (pair_send, pair_recv, hop_send, hop_recv))

    def compute(distance):
        rows = pl.ds((distance - 1) * 4 * tok, 4 * tok)
        span = min(512, width)

        @pl.loop(0, width // span)
        def _(j):
            part = pl.ds(pl.multiple_of(j * span, span), span)
            share[rows, part] = narrow(
                jnp.dot(columns[rows, :], weight_ref[:, part], preferred_element_type=jnp.float32)
            )

    for distance in range(reach, 0, -1):
        for way, far, other in partners:
            if far == distance or (far == 0 and distance == reach):
                piece(way, far, other).wait_recv()
        compute(distance)
        reducing.start_pair(distance)
        if distance == reach:
            reducing.start_pair(0)
            reducing.finish_pair(reach)
            reducing.late()
            reducing.finish_pair(0)
        else:
            reducing.finish_pair(distance)
            if distance == reach - 1:
                reducing.early()
    reducing.run(
        lambda rows, total: narrow(wide(rows_ref[rows, :]) + jax.nn.silu(total)), out_ref
    )
    for copy in sent:
        copy.wait_send()


def merge(devices, number, after_first, merged_in, weight):
    tok, width = after_first.shape
    depth = weight.shape[0]
    pieces = merged_in.reshape(tok, devices, depth).transpose(1, 0, 2)
    vmem = pl.BlockSpec(memory_space=pltpu.VMEM)
    return pl.pallas_call(
        functools.partial(merge_kernel, devices),
        out_shape=jax.ShapeDtypeStruct((tok, width), jnp.bfloat16),
        in_specs=[vmem] * 3,
        out_specs=vmem,
        scratch_shapes=[pltpu.VMEM((devices * tok, depth), jnp.bfloat16)]
        + reduce_scratch(devices, tok, width)
        + [
            pltpu.SemaphoreType.DMA((devices,)),
            pltpu.SemaphoreType.DMA((devices,)),
            pltpu.SemaphoreType.DMA,
        ],
        compiler_params=pltpu.CompilerParams(
            collective_id=number, has_side_effects=True, vmem_limit_bytes=VMEM_LIMIT
        ),
    )(pieces, after_first, weight)


def rms_scale(values, gain_vec):
    widened = values.astype(jnp.float32)
    inverse_rms = lax.rsqrt(jnp.mean(widened * widened, axis=-1, keepdims=True) + EPSILON)
    return (widened * inverse_rms * gain_vec).astype(jnp.bfloat16)


def dense_gates(routes, gates, experts):
    hit = routes[:, :, None] == jnp.arange(experts, dtype=jnp.int32)[None, None, :]
    return jnp.sum(jnp.where(hit, gates[:, :, None], 0.0), axis=1)


def plain_layer(devices, rows, routes, gates, gate_up, down):
    dense = lax.all_gather(dense_gates(routes, gates, devices), "inner", axis=0, tiled=True)
    column = lax.dynamic_slice_in_dim(dense, lax.axis_index("inner"), 1, axis=1)
    everyone = lax.all_gather(rows, "inner", axis=0, tiled=True)
    width = down.shape[1]
    projected = jnp.dot(everyone, gate_up[0], preferred_element_type=jnp.float32)
    inner = narrow(jax.nn.silu(projected[:, :width]) * projected[:, width:])
    share = narrow(jnp.dot(inner, down[0], preferred_element_type=jnp.float32) * column)
    total = lax.psum_scatter(share, "inner", scatter_dimension=0, tiled=True)
    return narrow(wide(rows) + wide(total))


def plain_merge(after_first, merged_in, weight):
    columns = lax.all_to_all(merged_in, "inner", split_axis=1, concat_axis=0, tiled=True)
    partial = narrow(jnp.dot(columns, weight, preferred_element_type=jnp.float32))
    merged = lax.psum_scatter(partial, "inner", scatter_dimension=0, tiled=True)
    return narrow(wide(after_first) + jax.nn.silu(wide(merged)))


def local(
    hidden_rows,
    token_embed,
    first_routes,
    first_gates,
    first_gate_up,
    first_down,
    second_routes,
    second_gates,
    second_gate_up,
    second_down,
    hidden_gain,
    embed_gain,
    merge_weight,
):
    devices = lax.axis_size("inner")
    tok, width = hidden_rows.shape
    fits = 3 * devices * tok * width * 2 <= VMEM_LIMIT // 3 and devices % 4 == 0
    if fits:
        layer = lambda number, *operands: routed_layer(devices, number, *operands)
        join = functools.partial(merge, devices, 1)
    else:
        layer = lambda number, *operands: plain_layer(devices, *operands)
        join = plain_merge
    after_first = layer(0, hidden_rows, first_routes, first_gates, first_gate_up, first_down)
    merged_in = jnp.concatenate(
        [rms_scale(after_first, hidden_gain), rms_scale(token_embed, embed_gain)], axis=1
    )
    after_merge = join(after_first, merged_in, merge_weight)
    return layer(2, after_merge, second_routes, second_gates, second_gate_up, second_down)


def solution(mesh):
    rows = P(("groups", "inner"), None)
    return jax.shard_map(
        local,
        mesh=mesh,
        in_specs=(
            rows, rows, rows, rows,
            P("inner", None, None),
            P("inner", None, None),
            rows, rows,
            P("inner", None, None),
            P("inner", None, None),
            P(),
            P(),
            P("inner", None),
        ),
        out_specs=rows,
        check_vma=False,
    )
```

```python
import functools

import jax
import jax.numpy as jnp
from jax import lax
from jax.experimental import pallas as pl
from jax.experimental.pallas import tpu as pltpu
from jax.sharding import PartitionSpec as P

EPSILON = 1e-06
LANES = 128
PARTS = 2
LAG = 5
VMEM_LIMIT = 60 * 1024 * 1024


class Ring:
    def __init__(self, devices, tok):
        self.devices, self.tok = devices, tok
        self.chips = devices // 2
        self.reach = self.chips // 2
        self.rise = self.chips // 2
        me = lax.axis_index("inner")
        chip = me // 2
        across = chip % 2
        along = chip // 2
        self.core = me % 2
        self.place = along * (1 - across) + (2 * self.rise - 1 - along) * across
        self.me = me

    def device(self, shift, other):
        place = (self.place + shift + self.chips) % self.chips
        across = place // self.rise
        along = place * (1 - across) + (2 * self.rise - 1 - place) * across
        core = self.core * (1 - other) + (1 - self.core) * other
        return (along * 2 + across) * 2 + core

    def row(self, way, distance, other):
        if distance == 0:
            return ((self.reach - 1) * 4 + 2 + other) * self.tok
        if distance == self.reach:
            return ((self.reach - 1) * 4 + other) * self.tok
        return ((distance - 1) * 4 + way * 2 + other) * self.tok

    def half(self, way, distance, other, k):
        part = self.tok // 2
        return pl.ds(self.row(way, distance, other) + k * part, part)

    def block(self, way, distance, other):
        return pl.ds(self.row(way, distance, other), self.tok)


def remote(src, dst, send, recv, device):
    return pltpu.make_async_remote_copy(
        src_ref=src, dst_ref=dst, send_sem=send, recv_sem=recv,
        device_id={"inner": device}, device_id_type=pl.DeviceIdType.MESH,
    )


def greet(devices):
    barrier = pltpu.get_barrier_semaphore()
    for device in devices:
        pl.semaphore_signal(
            barrier, inc=1, device_id={"inner": device}, device_id_type=pl.DeviceIdType.MESH
        )
    pl.semaphore_wait(barrier, len(devices))


def wide(values):
    return values.astype(jnp.float32)


def narrow(values):
    return values.astype(jnp.bfloat16)


class Reduce:
    def __init__(self, ring, bufs, part):
        share, paired, arrived, pair_send, pair_recv, send, recv = bufs
        self.ring, self.part = ring, part
        self.share, self.paired, self.arrived = share.at[part], paired.at[part], arrived.at[part]
        self.pair_send, self.pair_recv, self.send, self.recv = pair_send, pair_recv, send, recv
        self.started = []

    def slots(self, distance):
        return (0,) if distance in (0, self.ring.reach) else (0, 1)

    def pair_copy(self, way, distance):
        ring = self.ring
        slot = ring.reach * 2 if distance == 0 else (distance - 1) * 2 + way
        here = self.paired.at[pl.ds(slot * ring.tok, ring.tok)]
        return remote(
            self.share.at[ring.block(way, distance, 1)], here,
            self.pair_send.at[self.part, slot], self.pair_recv.at[self.part, slot],
            ring.device(0, 1),
        ), here

    def start_pair(self, distance):
        for way in self.slots(distance):
            copy, _ = self.pair_copy(way, distance)
            copy.start()
            self.started.append(copy)

    def finish_pair(self, distance):
        for way in self.slots(distance):
            copy, here = self.pair_copy(way, distance)
            copy.wait_recv()
            rows = self.ring.block(way, distance, 0)
            self.share[rows, :] = narrow(wide(self.share[rows, :]) + wide(here[...]))

    def hop(self, way, distance, k):
        ring = self.ring
        rows = ring.tok // 2
        slot = (way * ring.reach + distance - 1) * 2 + k
        landing = self.arrived.at[pl.ds(slot * rows, rows)]
        return remote(
            self.share.at[ring.half(1 - way, distance, 0, k)], landing,
            self.send.at[self.part, slot], self.recv.at[self.part, slot],
            ring.device(1 - 2 * way, 0),
        ), landing

    def start_hop(self, way, distance, k):
        copy, _ = self.hop(way, distance, k)
        copy.start()
        self.started.append(copy)

    def step(self, way, distance, k):
        copy, landing = self.hop(way, distance + 1, k)
        copy.wait_recv()
        rows = self.ring.half(1 - way, distance, 0, k)
        self.share[rows, :] = narrow(wide(self.share[rows, :]) + wide(landing[...]))
        self.start_hop(way, distance, k)

    def early(self):
        reach = self.ring.reach
        if reach > 1:
            for way in (0, 1):
                self.start_hop(way, reach - 1, 1 - way)

    def late(self):
        for way in (0, 1):
            self.start_hop(way, self.ring.reach, way)

    def run(self):
        reach = self.ring.reach
        for distance in range(reach - 1, 0, -1):
            yield
            for way in (0, 1):
                self.step(way, distance, way)
            if distance > 1:
                for way in (0, 1):
                    self.step(way, distance - 1, 1 - way)
        yield
        totals = []
        for k in (0, 1):
            total = wide(self.share[self.ring.half(0, 0, 0, k), :])
            for way in (0, 1):
                if k == way or reach > 1:
                    copy, landing = self.hop(way, 1, k)
                    copy.wait_recv()
                    total = total + wide(landing[...])
            totals.append(total)
        return jnp.concatenate(totals, axis=0)


def reduce_scratch(devices, tok, width):
    reach = devices // 4
    return [
        pltpu.VMEM((PARTS, devices * tok, width), jnp.bfloat16),
        pltpu.VMEM((PARTS, (2 * reach + 1) * tok, width), jnp.bfloat16),
        pltpu.VMEM((PARTS, 2 * reach * tok, width), jnp.bfloat16),
        pltpu.SemaphoreType.DMA((PARTS, 2 * reach + 1)),
        pltpu.SemaphoreType.DMA((PARTS, 2 * reach + 1)),
        pltpu.SemaphoreType.DMA((PARTS, 4 * reach)),
        pltpu.SemaphoreType.DMA((PARTS, 4 * reach)),
    ]


def gather_scratch(devices, tok, width):
    reach = devices // 4
    return [
        pltpu.VMEM((PARTS, devices * tok, width), jnp.bfloat16),
        pltpu.SemaphoreType.DMA((PARTS, 4 * reach)),
        pltpu.SemaphoreType.DMA((PARTS, 4 * reach)),
        pltpu.SemaphoreType.DMA((PARTS, 4 * reach + 1)),
        pltpu.SemaphoreType.DMA((PARTS, 4 * reach + 1)),
    ]


def normed(values, gain):
    widened = wide(values)
    inverse_rms = lax.rsqrt(jnp.mean(widened * widened, axis=-1, keepdims=True) + EPSILON)
    return narrow(widened * inverse_rms * gain)


def gate_lanes(devices, lanes, tables):
    rows = tables[0][0].shape[0]
    lane = lax.broadcasted_iota(jnp.int32, (rows, lanes), 1)
    packed = jnp.zeros((rows, lanes), jnp.float32)
    for layer, (routes, gates) in enumerate(tables):
        base = 2 * layer * devices
        high_part = (lane >= base) & (lane < base + devices)
        low_part = (lane >= base + devices) & (lane < base + 2 * devices)
        expert = jnp.where(high_part, lane - base, lane - base - devices)
        dense = jnp.zeros((rows, lanes), jnp.float32)
        for k in range(routes.shape[1]):
            dense = dense + jnp.where(expert == routes[:, k : k + 1], gates[:, k : k + 1], 0.0)
        high = wide(narrow(dense))
        packed = jnp.where(high_part, high, jnp.where(low_part, dense - high, packed))
    return narrow(packed)


def block_kernel(devices, *refs):
    (hidden_ref, embed_ref, routes1, gates1, routes2, gates2, hidden_gain, embed_gain,
     gu1_ref, down1_ref, weight_ref, gu2_ref, down2_ref, out_ref) = refs[:14]
    scratch = list(refs[14:])
    take = lambda count: [scratch.pop(0) for _ in range(count)]
    gu1, down1, weight, gu2, down2, load_sem = take(6)
    packed, after_first, after_merge, pieces, columns, inner = take(6)
    piece_send, piece_recv, own_sem = take(3)
    gather1, gather2 = take(5), take(5)
    reduce1, reduce2, reduce3 = take(7), take(7), take(7)
    rows_all, width = hidden_ref.shape
    tok = rows_all // PARTS
    hidden = down1.shape[0]
    depth = weight.shape[0]
    lanes = packed.shape[1] - width
    ring = Ring(devices, tok)
    reach = ring.reach

    loads = [
        pltpu.make_async_copy(source, target, load_sem.at[i])
        for i, (source, target) in enumerate(
            [(gu1_ref.at[0], gu1), (down1_ref.at[0], down1), (weight_ref, weight),
             (gu2_ref.at[0], gu2), (down2_ref.at[0], down2)]
        )
    ]
    for load in loads:
        load.start()
    waiting = list(range(5))

    def need(*which):
        for i in which:
            if i in waiting:
                waiting.remove(i)
                loads[i].wait()

    packed[:, :width] = hidden_ref[...]
    packed[:, width:] = gate_lanes(
        devices, lanes, [(routes1[...], gates1[...]), (routes2[...], gates2[...])]
    )

    partners = [(0, 0, 1)]
    for distance in range(1, reach + 1):
        for other in (0, 1):
            partners.append((0, distance, other))
            if distance < reach:
                partners.append((1, distance, other))

    def target_of(way, distance, other):
        return ring.device(distance * (1 - 2 * way), other)

    greet([target_of(*partner) for partner in partners])
    started = []

    def begin(copy):
        copy.start()
        started.append(copy)

    def layer(part, source, bufs, first, reduce_bufs, load_ids, gu, down):
        everyone, send, recv, sib_send, sib_recv = bufs
        everyone = everyone.at[part]
        own_rows = pl.ds(part * tok, tok)

        def ring_copy(way, distance, k):
            slot = (way * reach + distance - 1) * 2 + k
            landing = everyone.at[ring.half(way, distance, 0, k)]
            origin = (
                source.at[pl.ds(part * tok + k * (tok // 2), tok // 2)]
                if distance == 1
                else everyone.at[ring.half(way, distance - 1, 0, k)]
            )
            return remote(
                origin, landing, send.at[part, slot], recv.at[part, slot],
                ring.device(1 - 2 * way, 0),
            )

        def sibling_copy(way, distance, k):
            if distance == 0:
                slot, origin, landing = 4 * reach, source.at[own_rows], everyone.at[ring.block(0, 0, 1)]
            else:
                slot = (way * reach + distance - 1) * 2 + k
                origin = everyone.at[ring.half(way, distance, 0, k)]
                landing = everyone.at[ring.half(way, distance, 1, k)]
            return remote(
                origin, landing, sib_send.at[part, slot], sib_recv.at[part, slot],
                ring.device(0, 1),
            )

        reducing = Reduce(ring, reduce_bufs, part)
        share = reducing.share
        gate_rows = gather1[0].at[part]

        def compute(distance):
            rows = pl.ds((distance - 1) * 4 * tok, 4 * tok)
            x = everyone.at[rows]
            step = min(256, hidden)

            @pl.loop(0, hidden // step)
            def _(j):
                left = pl.ds(pl.multiple_of(j * step, step), step)
                right = pl.ds(pl.multiple_of(hidden + j * step, step), step)
                g = jnp.dot(x[:, :width], gu[:, left], preferred_element_type=jnp.float32)
                u = jnp.dot(x[:, :width], gu[:, right], preferred_element_type=jnp.float32)
                inner[:, left] = narrow(jax.nn.silu(g) * u)

            lane = lax.broadcasted_iota(jnp.int32, (4 * tok, lanes), 1)
            mine = (lane == ring.me + first * devices) | (lane == ring.me + (first + 1) * devices)
            gate = jnp.sum(
                jnp.where(mine, wide(gate_rows[rows, width:]), 0.0), axis=1, keepdims=True
            )
            span = min(512, width)

            @pl.loop(0, width // span)
            def _(j):
                part_columns = pl.ds(pl.multiple_of(j * span, span), span)
                out = jnp.dot(inner[...], down[:, part_columns], preferred_element_type=jnp.float32)
                share[rows, part_columns] = narrow(out * gate)

        def streams(distance):
            for short in (0, 1):
                if not (short and distance == reach):
                    for way in (0, 1):
                        yield way, (1 - way if short else way), short

        for way, k, _ in streams(1):
            begin(ring_copy(way, 1, k))
        begin(sibling_copy(0, 0, 0))
        everyone[ring.block(0, 0, 0), :] = source[own_rows, :]
        for distance in range(1, reach + 1):
            yield
            for way, k, short in streams(distance):
                ring_copy(way, distance, k).wait_recv()
                if distance < reach and not (short and distance == reach - 1):
                    begin(ring_copy(way, distance + 1, k))
                begin(sibling_copy(way, distance, k))
            if distance == 1:
                need(*load_ids)
            else:
                for way, k, _ in streams(distance - 1):
                    sibling_copy(way, distance - 1, k).wait_recv()
                compute(distance - 1)
                reducing.start_pair(distance - 1)
        for distance in range(1, reach):
            reducing.finish_pair(distance)
        reducing.early()
        yield
        for way, k, _ in streams(reach):
            sibling_copy(way, reach, k).wait_recv()
        sibling_copy(0, 0, 0).wait_recv()
        compute(reach)
        reducing.start_pair(reach)
        reducing.start_pair(0)
        reducing.finish_pair(reach)
        reducing.late()
        reducing.finish_pair(0)
        total = yield from reducing.run()
        started.extend(reducing.started)
        return total

    def merged(part):
        here, landed = pieces.at[part], columns.at[part]

        def piece(way, distance, other):
            target = target_of(way, distance, other)
            slot = ring.row(way, distance, other) // tok
            return remote(
                here.at[target], landed.at[ring.block(way, distance, other)],
                piece_send.at[part, slot], piece_recv.at[part, slot], target,
            )

        for partner in reversed(partners):
            begin(piece(*partner))
        own = pltpu.make_async_copy(
            here.at[ring.me], landed.at[ring.block(0, 0, 0)], own_sem.at[part]
        )
        own.start()
        need(2)
        reducing = Reduce(ring, reduce2, part)
        share = reducing.share
        for distance in range(reach, 0, -1):
            if distance % 2 == 0:
                yield
            if distance == reach:
                own.wait()
            for way, far, other in partners:
                if far == distance or (far == 0 and distance == reach):
                    piece(way, far, other).wait_recv()
            rows = pl.ds((distance - 1) * 4 * tok, 4 * tok)
            span = min(512, width)

            @pl.loop(0, width // span)
            def _(j):
                cut = pl.ds(pl.multiple_of(j * span, span), span)
                share[rows, cut] = narrow(
                    jnp.dot(landed[rows, :], weight[:, cut], preferred_element_type=jnp.float32)
                )

            reducing.start_pair(distance)
            if distance == reach:
                reducing.start_pair(0)
                reducing.finish_pair(reach)
                reducing.late()
                reducing.finish_pair(0)
            else:
                reducing.finish_pair(distance)
                if distance == reach - 1:
                    reducing.early()
        total = yield from reducing.run()
        started.extend(reducing.started)
        return total

    def scatter_pieces(part, values, at):
        for j in range(width // depth):
            pieces[part, at + j] = values[:, j * depth : (j + 1) * depth]

    def pipeline(part):
        rows = pl.ds(part * tok, tok)
        total = yield from layer(part, packed, gather1, 0, reduce1, (0, 1), gu1, down1)
        first = narrow(wide(hidden_ref[rows, :]) + total)
        after_first[rows, :] = first
        scatter_pieces(part, normed(first, hidden_gain[...]), 0)
        total = yield from merged(part)
        after_merge[rows, :] = narrow(wide(after_first[rows, :]) + jax.nn.silu(total))
        total = yield from layer(part, after_merge, gather2, 2, reduce3, (3, 4), gu2, down2)
        out_ref[rows, :] = narrow(wide(after_merge[rows, :]) + total)

    lines = [pipeline(part) for part in range(PARTS)]
    done = object()
    tick = 0
    while lines:
        for at, line in enumerate(list(lines)):
            if tick >= at * LAG or len(lines) < PARTS:
                if next(line, done) is done:
                    lines.remove(line)
        if tick == 0:
            for part in range(PARTS):
                rows = pl.ds(part * tok, tok)
                scatter_pieces(part, normed(embed_ref[rows, :], embed_gain[...]), width // depth)
        tick += 1
    for copy in started:
        copy.wait_send()


def fused(hidden_rows, token_embed, first_routes, first_gates, first_gate_up, first_down,
          second_routes, second_gates, second_gate_up, second_down, hidden_gain, embed_gain,
          merge_weight):
    devices = lax.axis_size("inner")
    rows, width = hidden_rows.shape
    tok = rows // PARTS
    hidden = first_down.shape[1]
    depth = merge_weight.shape[0]
    lanes = -(-4 * devices // LANES) * LANES
    vmem = pl.BlockSpec(memory_space=pltpu.VMEM)
    hbm = pl.BlockSpec(memory_space=pl.ANY)
    bf16 = jnp.bfloat16
    scratch = [
        pltpu.VMEM(first_gate_up.shape[1:], bf16),
        pltpu.VMEM(first_down.shape[1:], bf16),
        pltpu.VMEM(merge_weight.shape, bf16),
        pltpu.VMEM(second_gate_up.shape[1:], bf16),
        pltpu.VMEM(second_down.shape[1:], bf16),
        pltpu.SemaphoreType.DMA((5,)),
        pltpu.VMEM((rows, width + lanes), bf16),
        pltpu.VMEM((rows, width), bf16),
        pltpu.VMEM((rows, width), bf16),
        pltpu.VMEM((PARTS, devices, tok, depth), bf16),
        pltpu.VMEM((PARTS, devices * tok, depth), bf16),
        pltpu.VMEM((4 * tok, hidden), bf16),
        pltpu.SemaphoreType.DMA((PARTS, devices)),
        pltpu.SemaphoreType.DMA((PARTS, devices)),
        pltpu.SemaphoreType.DMA((PARTS,)),
    ]
    scratch += gather_scratch(devices, tok, width + lanes) + gather_scratch(devices, tok, width)
    for _ in range(3):
        scratch += reduce_scratch(devices, tok, width)
    return pl.pallas_call(
        functools.partial(block_kernel, devices),
        out_shape=jax.ShapeDtypeStruct((rows, width), bf16),
        in_specs=[vmem] * 8 + [hbm] * 5,
        out_specs=vmem,
        scratch_shapes=scratch,
        compiler_params=pltpu.CompilerParams(
            collective_id=0, has_side_effects=True, vmem_limit_bytes=VMEM_LIMIT
        ),
    )(hidden_rows, token_embed, first_routes, first_gates, second_routes, second_gates,
      hidden_gain[None], embed_gain[None], first_gate_up, first_down, merge_weight,
      second_gate_up, second_down)


def rms_scale(values, gain_vec):
    widened = values.astype(jnp.float32)
    inverse_rms = lax.rsqrt(jnp.mean(widened * widened, axis=-1, keepdims=True) + EPSILON)
    return (widened * inverse_rms * gain_vec).astype(jnp.bfloat16)


def dense_gates(routes, gates, experts):
    hit = routes[:, :, None] == jnp.arange(experts, dtype=jnp.int32)[None, None, :]
    return jnp.sum(jnp.where(hit, gates[:, :, None], 0.0), axis=1)


def plain_layer(devices, rows, routes, gates, gate_up, down):
    dense = lax.all_gather(dense_gates(routes, gates, devices), "inner", axis=0, tiled=True)
    column = lax.dynamic_slice_in_dim(dense, lax.axis_index("inner"), 1, axis=1)
    everyone = lax.all_gather(rows, "inner", axis=0, tiled=True)
    width = down.shape[1]
    projected = jnp.dot(everyone, gate_up[0], preferred_element_type=jnp.float32)
    inner = narrow(jax.nn.silu(projected[:, :width]) * projected[:, width:])
    share = narrow(jnp.dot(inner, down[0], preferred_element_type=jnp.float32) * column)
    total = lax.psum_scatter(share, "inner", scatter_dimension=0, tiled=True)
    return narrow(wide(rows) + wide(total))


def plain_merge(after_first, merged_in, weight):
    columns = lax.all_to_all(merged_in, "inner", split_axis=1, concat_axis=0, tiled=True)
    partial = narrow(jnp.dot(columns, weight, preferred_element_type=jnp.float32))
    merged = lax.psum_scatter(partial, "inner", scatter_dimension=0, tiled=True)
    return narrow(wide(after_first) + jax.nn.silu(wide(merged)))


def unfused(hidden_rows, token_embed, first_routes, first_gates, first_gate_up, first_down,
            second_routes, second_gates, second_gate_up, second_down, hidden_gain, embed_gain,
            merge_weight):
    devices = lax.axis_size("inner")
    after_first = plain_layer(
        devices, hidden_rows, first_routes, first_gates, first_gate_up, first_down
    )
    merged_in = jnp.concatenate(
        [rms_scale(after_first, hidden_gain), rms_scale(token_embed, embed_gain)], axis=1
    )
    after_merge = plain_merge(after_first, merged_in, merge_weight)
    return plain_layer(devices, after_merge, second_routes, second_gates, second_gate_up, second_down)


def local(hidden_rows, *others):
    devices = lax.axis_size("inner")
    tok, width = hidden_rows.shape
    fits = 12 * devices * tok * width * 2 <= VMEM_LIMIT and devices % 4 == 0 and tok % 32 == 0
    return (fused if fits else unfused)(hidden_rows, *others)


def solution(mesh):
    rows = P(("groups", "inner"), None)
    return jax.shard_map(
        local,
        mesh=mesh,
        in_specs=(
            rows, rows, rows, rows,
            P("inner", None, None),
            P("inner", None, None),
            rows, rows,
            P("inner", None, None),
            P("inner", None, None),
            P(),
            P(),
            P("inner", None),
        ),
        out_specs=rows,
        check_vma=False,
    )
```

```python
import functools

import jax
import jax.numpy as jnp
from jax import lax
from jax.experimental import pallas as pl
from jax.experimental.pallas import tpu as pltpu
from jax.sharding import PartitionSpec as P

EPSILON = 1e-06
LANES = 128
PARTS = 1
LAG = 0
VMEM_LIMIT = 60 * 1024 * 1024


class Ring:
    def __init__(self, devices, tok):
        self.devices, self.tok = devices, tok
        self.chips = devices // 2
        self.reach = self.chips // 2
        self.rise = self.chips // 2
        me = lax.axis_index("inner")
        chip = me // 2
        across = chip % 2
        along = chip // 2
        self.core = me % 2
        self.place = along * (1 - across) + (2 * self.rise - 1 - along) * across
        self.me = me

    def device(self, shift, other):
        place = (self.place + shift + self.chips) % self.chips
        across = place // self.rise
        along = place * (1 - across) + (2 * self.rise - 1 - place) * across
        core = self.core * (1 - other) + (1 - self.core) * other
        return (along * 2 + across) * 2 + core

    def row(self, way, distance, other):
        if distance == 0:
            return ((self.reach - 1) * 4 + 2 + other) * self.tok
        if distance == self.reach:
            return ((self.reach - 1) * 4 + other) * self.tok
        return ((distance - 1) * 4 + way * 2 + other) * self.tok

    def half(self, way, distance, other, k):
        part = self.tok // 2
        return pl.ds(self.row(way, distance, other) + k * part, part)

    def block(self, way, distance, other):
        return pl.ds(self.row(way, distance, other), self.tok)


def remote(src, dst, send, recv, device):
    return pltpu.make_async_remote_copy(
        src_ref=src, dst_ref=dst, send_sem=send, recv_sem=recv,
        device_id={"inner": device}, device_id_type=pl.DeviceIdType.MESH,
    )


def greet(devices):
    barrier = pltpu.get_barrier_semaphore()
    for device in devices:
        pl.semaphore_signal(
            barrier, inc=1, device_id={"inner": device}, device_id_type=pl.DeviceIdType.MESH
        )
    pl.semaphore_wait(barrier, len(devices))


def wide(values):
    return values.astype(jnp.float32)


def narrow(values):
    return values.astype(jnp.bfloat16)


class Reduce:
    def __init__(self, ring, bufs, part):
        share, paired, arrived, pair_send, pair_recv, send, recv = bufs
        self.ring, self.part = ring, part
        self.share, self.paired, self.arrived = share.at[part], paired.at[part], arrived.at[part]
        self.pair_send, self.pair_recv, self.send, self.recv = pair_send, pair_recv, send, recv
        self.started = []

    def slots(self, distance):
        return (0,) if distance in (0, self.ring.reach) else (0, 1)

    def pair_copy(self, way, distance):
        ring = self.ring
        slot = ring.reach * 2 if distance == 0 else (distance - 1) * 2 + way
        here = self.paired.at[pl.ds(slot * ring.tok, ring.tok)]
        return remote(
            self.share.at[ring.block(way, distance, 1)], here,
            self.pair_send.at[self.part, slot], self.pair_recv.at[self.part, slot],
            ring.device(0, 1),
        ), here

    def start_pair(self, distance):
        for way in self.slots(distance):
            copy, _ = self.pair_copy(way, distance)
            copy.start()
            self.started.append(copy)

    def finish_pair(self, distance):
        for way in self.slots(distance):
            copy, here = self.pair_copy(way, distance)
            copy.wait_recv()
            rows = self.ring.block(way, distance, 0)
            self.share[rows, :] = narrow(wide(self.share[rows, :]) + wide(here[...]))

    def hop(self, way, distance, k):
        ring = self.ring
        rows = ring.tok // 2
        slot = (way * ring.reach + distance - 1) * 2 + k
        landing = self.arrived.at[pl.ds(slot * rows, rows)]
        return remote(
            self.share.at[ring.half(1 - way, distance, 0, k)], landing,
            self.send.at[self.part, slot], self.recv.at[self.part, slot],
            ring.device(1 - 2 * way, 0),
        ), landing

    def start_hop(self, way, distance, k):
        copy, _ = self.hop(way, distance, k)
        copy.start()
        self.started.append(copy)

    def step(self, way, distance, k):
        copy, landing = self.hop(way, distance + 1, k)
        copy.wait_recv()
        rows = self.ring.half(1 - way, distance, 0, k)
        self.share[rows, :] = narrow(wide(self.share[rows, :]) + wide(landing[...]))
        self.start_hop(way, distance, k)

    def early(self):
        reach = self.ring.reach
        if reach > 1:
            for way in (0, 1):
                self.start_hop(way, reach - 1, 1 - way)

    def late(self):
        for way in (0, 1):
            self.start_hop(way, self.ring.reach, way)

    def run(self):
        reach = self.ring.reach
        for distance in range(reach - 1, 0, -1):
            yield
            for way in (0, 1):
                self.step(way, distance, way)
            if distance > 1:
                for way in (0, 1):
                    self.step(way, distance - 1, 1 - way)
        yield
        totals = []
        for k in (0, 1):
            total = wide(self.share[self.ring.half(0, 0, 0, k), :])
            for way in (0, 1):
                if k == way or reach > 1:
                    copy, landing = self.hop(way, 1, k)
                    copy.wait_recv()
                    total = total + wide(landing[...])
            totals.append(total)
        return jnp.concatenate(totals, axis=0)


def reduce_scratch(devices, tok, width):
    reach = devices // 4
    return [
        pltpu.VMEM((PARTS, devices * tok, width), jnp.bfloat16),
        pltpu.VMEM((PARTS, (2 * reach + 1) * tok, width), jnp.bfloat16),
        pltpu.VMEM((PARTS, 2 * reach * tok, width), jnp.bfloat16),
        pltpu.SemaphoreType.DMA((PARTS, 2 * reach + 1)),
        pltpu.SemaphoreType.DMA((PARTS, 2 * reach + 1)),
        pltpu.SemaphoreType.DMA((PARTS, 4 * reach)),
        pltpu.SemaphoreType.DMA((PARTS, 4 * reach)),
    ]


def gather_scratch(devices, tok, width):
    reach = devices // 4
    return [
        pltpu.VMEM((PARTS, devices * tok, width), jnp.bfloat16),
        pltpu.SemaphoreType.DMA((PARTS, 4 * reach)),
        pltpu.SemaphoreType.DMA((PARTS, 4 * reach)),
        pltpu.SemaphoreType.DMA((PARTS, 4 * reach + 1)),
        pltpu.SemaphoreType.DMA((PARTS, 4 * reach + 1)),
    ]


def normed(values, gain):
    widened = wide(values)
    inverse_rms = lax.rsqrt(jnp.mean(widened * widened, axis=-1, keepdims=True) + EPSILON)
    return narrow(widened * inverse_rms * gain)


def gate_lanes(devices, lanes, tables):
    rows = tables[0][0].shape[0]
    lane = lax.broadcasted_iota(jnp.int32, (rows, lanes), 1)
    packed = jnp.zeros((rows, lanes), jnp.float32)
    for layer, (routes, gates) in enumerate(tables):
        base = 2 * layer * devices
        high_part = (lane >= base) & (lane < base + devices)
        low_part = (lane >= base + devices) & (lane < base + 2 * devices)
        expert = jnp.where(high_part, lane - base, lane - base - devices)
        dense = jnp.zeros((rows, lanes), jnp.float32)
        for k in range(routes.shape[1]):
            dense = dense + jnp.where(expert == routes[:, k : k + 1], gates[:, k : k + 1], 0.0)
        high = wide(narrow(dense))
        packed = jnp.where(high_part, high, jnp.where(low_part, dense - high, packed))
    return narrow(packed)


def block_kernel(devices, *refs):
    (hidden_ref, embed_ref, routes1, gates1, routes2, gates2, hidden_gain, embed_gain,
     gu1_ref, down1_ref, weight_ref, gu2_ref, down2_ref, out_ref) = refs[:14]
    scratch = list(refs[14:])
    take = lambda count: [scratch.pop(0) for _ in range(count)]
    gu1, down1, weight, gu2, down2, load_sem = take(6)
    packed, after_first, after_merge, pieces, columns, inner = take(6)
    piece_send, piece_recv, own_sem = take(3)
    gather1, gather2 = take(5), take(5)
    reduce1, reduce2, reduce3 = take(7), take(7), take(7)
    rows_all, width = hidden_ref.shape
    tok = rows_all // PARTS
    hidden = down1.shape[0]
    depth = weight.shape[0]
    lanes = packed.shape[1] - width
    ring = Ring(devices, tok)
    reach = ring.reach

    loads = [
        pltpu.make_async_copy(source, target, load_sem.at[i])
        for i, (source, target) in enumerate(
            [(gu1_ref.at[0], gu1), (down1_ref.at[0], down1), (weight_ref, weight),
             (gu2_ref.at[0], gu2), (down2_ref.at[0], down2)]
        )
    ]
    for load in loads:
        load.start()
    waiting = list(range(5))

    def need(*which):
        for i in which:
            if i in waiting:
                waiting.remove(i)
                loads[i].wait()

    packed[:, :width] = hidden_ref[...]
    packed[:, width:] = gate_lanes(
        devices, lanes, [(routes1[...], gates1[...]), (routes2[...], gates2[...])]
    )

    partners = [(0, 0, 1)]
    for distance in range(1, reach + 1):
        for other in (0, 1):
            partners.append((0, distance, other))
            if distance < reach:
                partners.append((1, distance, other))

    def target_of(way, distance, other):
        return ring.device(distance * (1 - 2 * way), other)

    greet([target_of(*partner) for partner in partners])
    started = []

    def begin(copy):
        copy.start()
        started.append(copy)

    def layer(part, source, bufs, first, reduce_bufs, load_ids, gu, down):
        everyone, send, recv, sib_send, sib_recv = bufs
        everyone = everyone.at[part]
        own_rows = pl.ds(part * tok, tok)

        def ring_copy(way, distance, k):
            slot = (way * reach + distance - 1) * 2 + k
            landing = everyone.at[ring.half(way, distance, 0, k)]
            origin = (
                source.at[pl.ds(part * tok + k * (tok // 2), tok // 2)]
                if distance == 1
                else everyone.at[ring.half(way, distance - 1, 0, k)]
            )
            return remote(
                origin, landing, send.at[part, slot], recv.at[part, slot],
                ring.device(1 - 2 * way, 0),
            )

        def sibling_copy(way, distance, k):
            if distance == 0:
                slot, origin, landing = 4 * reach, source.at[own_rows], everyone.at[ring.block(0, 0, 1)]
            else:
                slot = (way * reach + distance - 1) * 2 + k
                origin = everyone.at[ring.half(way, distance, 0, k)]
                landing = everyone.at[ring.half(way, distance, 1, k)]
            return remote(
                origin, landing, sib_send.at[part, slot], sib_recv.at[part, slot],
                ring.device(0, 1),
            )

        reducing = Reduce(ring, reduce_bufs, part)
        share = reducing.share
        gate_rows = gather1[0].at[part]

        def span_of(distance):
            if distance == 0:
                return ring.row(0, 0, 0), 2 * tok
            return (distance - 1) * 4 * tok, (2 if distance == reach else 4) * tok

        def up(distance):
            first_row, count = span_of(distance)
            rows = pl.ds(first_row, count)
            step = min(256, hidden)

            @pl.loop(0, hidden // step)
            def _(j):
                left = pl.ds(pl.multiple_of(j * step, step), step)
                right = pl.ds(pl.multiple_of(hidden + j * step, step), step)
                x = everyone[rows, :width]
                g = jnp.dot(x, gu[:, left], preferred_element_type=jnp.float32)
                u = jnp.dot(x, gu[:, right], preferred_element_type=jnp.float32)
                inner[part, :count, left] = narrow(jax.nn.silu(g) * u)

        def finish(distance):
            first_row, count = span_of(distance)
            rows = pl.ds(first_row, count)
            lane = lax.broadcasted_iota(jnp.int32, (count, lanes), 1)
            mine = (lane == ring.me + first * devices) | (lane == ring.me + (first + 1) * devices)
            gate = jnp.sum(
                jnp.where(mine, wide(gate_rows[rows, width:]), 0.0), axis=1, keepdims=True
            )
            span = min(512, width)

            @pl.loop(0, width // span)
            def _(j):
                cut = pl.ds(pl.multiple_of(j * span, span), span)
                out = jnp.dot(
                    inner[part, :count, :], down[:, cut], preferred_element_type=jnp.float32
                )
                share[rows, cut] = narrow(out * gate)

            reducing.start_pair(distance)

        def streams(distance):
            for short in (0, 1):
                if not (short and distance == reach):
                    for way in (0, 1):
                        yield way, (1 - way if short else way), short

        for way, k, _ in streams(1):
            begin(ring_copy(way, 1, k))
        begin(sibling_copy(0, 0, 0))
        everyone[ring.block(0, 0, 0), :] = source[own_rows, :]

        def pass_on(distance, short):
            for way, k, which in streams(distance):
                if which == short:
                    ring_copy(way, distance, k).wait_recv()
                    if distance < reach and not (short and distance == reach - 1):
                        begin(ring_copy(way, distance + 1, k))
                    begin(sibling_copy(way, distance, k))

        def from_sibling(distance):
            if distance == 0:
                sibling_copy(0, 0, 0).wait_recv()
            else:
                for way, k, _ in streams(distance):
                    sibling_copy(way, distance, k).wait_recv()

        yield
        need(*load_ids)
        from_sibling(0)
        up(0)
        for distance in range(1, reach):
            yield
            pass_on(distance, 0)
            if distance == 1:
                finish(0)
            else:
                from_sibling(distance - 1)
                up(distance - 1)
            yield
            pass_on(distance, 1)
            if distance > 1:
                finish(distance - 1)
                reducing.finish_pair(distance - 2)
        yield
        if reach > 1:
            from_sibling(reach - 1)
            up(reach - 1)
        yield
        pass_on(reach, 0)
        if reach > 1:
            finish(reach - 1)
            reducing.finish_pair(reach - 2)
        yield
        from_sibling(reach)
        up(reach)
        if reach > 1:
            reducing.finish_pair(reach - 1)
            reducing.early()
        finish(reach)
        yield
        reducing.finish_pair(reach)
        reducing.late()
        total = yield from reducing.run()
        started.extend(reducing.started)
        return total

    def merged(part):
        here, landed = pieces.at[part], columns.at[part]

        def piece(way, distance, other):
            target = target_of(way, distance, other)
            slot = ring.row(way, distance, other) // tok
            return remote(
                here.at[target], landed.at[ring.block(way, distance, other)],
                piece_send.at[part, slot], piece_recv.at[part, slot], target,
            )

        for partner in reversed(partners):
            begin(piece(*partner))
        own = pltpu.make_async_copy(
            here.at[ring.me], landed.at[ring.block(0, 0, 0)], own_sem.at[part]
        )
        own.start()
        need(2)
        reducing = Reduce(ring, reduce2, part)
        share = reducing.share
        for distance in range(reach, 0, -1):
            if distance % 2 == 0:
                yield
            if distance == reach:
                own.wait()
            for way, far, other in partners:
                if far == distance or (far == 0 and distance == reach):
                    piece(way, far, other).wait_recv()
            rows = pl.ds((distance - 1) * 4 * tok, 4 * tok)
            span = min(512, width)

            @pl.loop(0, width // span)
            def _(j):
                cut = pl.ds(pl.multiple_of(j * span, span), span)
                share[rows, cut] = narrow(
                    jnp.dot(landed[rows, :], weight[:, cut], preferred_element_type=jnp.float32)
                )

            reducing.start_pair(distance)
            if distance == reach:
                reducing.start_pair(0)
                reducing.finish_pair(reach)
                reducing.late()
                reducing.finish_pair(0)
            else:
                reducing.finish_pair(distance)
                if distance == reach - 1:
                    reducing.early()
        total = yield from reducing.run()
        started.extend(reducing.started)
        return total

    def scatter_pieces(part, values, at):
        for j in range(width // depth):
            pieces[part, at + j] = values[:, j * depth : (j + 1) * depth]

    def pipeline(part):
        rows = pl.ds(part * tok, tok)
        total = yield from layer(part, packed, gather1, 0, reduce1, (0, 1), gu1, down1)
        first = narrow(wide(hidden_ref[rows, :]) + total)
        after_first[rows, :] = first
        scatter_pieces(part, normed(first, hidden_gain[...]), 0)
        total = yield from merged(part)
        after_merge[rows, :] = narrow(wide(after_first[rows, :]) + jax.nn.silu(total))
        total = yield from layer(part, after_merge, gather2, 2, reduce3, (3, 4), gu2, down2)
        out_ref[rows, :] = narrow(wide(after_merge[rows, :]) + total)

    lines = [pipeline(part) for part in range(PARTS)]
    done = object()
    tick = 0
    while lines:
        for at, line in enumerate(list(lines)):
            if tick >= at * LAG or len(lines) < PARTS:
                if next(line, done) is done:
                    lines.remove(line)
        if tick == 0:
            for part in range(PARTS):
                rows = pl.ds(part * tok, tok)
                scatter_pieces(part, normed(embed_ref[rows, :], embed_gain[...]), width // depth)
        tick += 1
    for copy in started:
        copy.wait_send()


def fused(hidden_rows, token_embed, first_routes, first_gates, first_gate_up, first_down,
          second_routes, second_gates, second_gate_up, second_down, hidden_gain, embed_gain,
          merge_weight):
    devices = lax.axis_size("inner")
    rows, width = hidden_rows.shape
    tok = rows // PARTS
    hidden = first_down.shape[1]
    depth = merge_weight.shape[0]
    lanes = -(-4 * devices // LANES) * LANES
    vmem = pl.BlockSpec(memory_space=pltpu.VMEM)
    hbm = pl.BlockSpec(memory_space=pl.ANY)
    bf16 = jnp.bfloat16
    scratch = [
        pltpu.VMEM(first_gate_up.shape[1:], bf16),
        pltpu.VMEM(first_down.shape[1:], bf16),
        pltpu.VMEM(merge_weight.shape, bf16),
        pltpu.VMEM(second_gate_up.shape[1:], bf16),
        pltpu.VMEM(second_down.shape[1:], bf16),
        pltpu.SemaphoreType.DMA((5,)),
        pltpu.VMEM((rows, width + lanes), bf16),
        pltpu.VMEM((rows, width), bf16),
        pltpu.VMEM((rows, width), bf16),
        pltpu.VMEM((PARTS, devices, tok, depth), bf16),
        pltpu.VMEM((PARTS, devices * tok, depth), bf16),
        pltpu.VMEM((PARTS, 4 * tok, hidden), bf16),
        pltpu.SemaphoreType.DMA((PARTS, devices)),
        pltpu.SemaphoreType.DMA((PARTS, devices)),
        pltpu.SemaphoreType.DMA((PARTS,)),
    ]
    scratch += gather_scratch(devices, tok, width + lanes) + gather_scratch(devices, tok, width)
    for _ in range(3):
        scratch += reduce_scratch(devices, tok, width)
    return pl.pallas_call(
        functools.partial(block_kernel, devices),
        out_shape=jax.ShapeDtypeStruct((rows, width), bf16),
        in_specs=[vmem] * 8 + [hbm] * 5,
        out_specs=vmem,
        scratch_shapes=scratch,
        compiler_params=pltpu.CompilerParams(
            collective_id=0, has_side_effects=True, vmem_limit_bytes=VMEM_LIMIT
        ),
    )(hidden_rows, token_embed, first_routes, first_gates, second_routes, second_gates,
      hidden_gain[None], embed_gain[None], first_gate_up, first_down, merge_weight,
      second_gate_up, second_down)


def rms_scale(values, gain_vec):
    widened = values.astype(jnp.float32)
    inverse_rms = lax.rsqrt(jnp.mean(widened * widened, axis=-1, keepdims=True) + EPSILON)
    return (widened * inverse_rms * gain_vec).astype(jnp.bfloat16)


def dense_gates(routes, gates, experts):
    hit = routes[:, :, None] == jnp.arange(experts, dtype=jnp.int32)[None, None, :]
    return jnp.sum(jnp.where(hit, gates[:, :, None], 0.0), axis=1)


def plain_layer(devices, rows, routes, gates, gate_up, down):
    dense = lax.all_gather(dense_gates(routes, gates, devices), "inner", axis=0, tiled=True)
    column = lax.dynamic_slice_in_dim(dense, lax.axis_index("inner"), 1, axis=1)
    everyone = lax.all_gather(rows, "inner", axis=0, tiled=True)
    width = down.shape[1]
    projected = jnp.dot(everyone, gate_up[0], preferred_element_type=jnp.float32)
    inner = narrow(jax.nn.silu(projected[:, :width]) * projected[:, width:])
    share = narrow(jnp.dot(inner, down[0], preferred_element_type=jnp.float32) * column)
    total = lax.psum_scatter(share, "inner", scatter_dimension=0, tiled=True)
    return narrow(wide(rows) + wide(total))


def plain_merge(after_first, merged_in, weight):
    columns = lax.all_to_all(merged_in, "inner", split_axis=1, concat_axis=0, tiled=True)
    partial = narrow(jnp.dot(columns, weight, preferred_element_type=jnp.float32))
    merged = lax.psum_scatter(partial, "inner", scatter_dimension=0, tiled=True)
    return narrow(wide(after_first) + jax.nn.silu(wide(merged)))


def unfused(hidden_rows, token_embed, first_routes, first_gates, first_gate_up, first_down,
            second_routes, second_gates, second_gate_up, second_down, hidden_gain, embed_gain,
            merge_weight):
    devices = lax.axis_size("inner")
    after_first = plain_layer(
        devices, hidden_rows, first_routes, first_gates, first_gate_up, first_down
    )
    merged_in = jnp.concatenate(
        [rms_scale(after_first, hidden_gain), rms_scale(token_embed, embed_gain)], axis=1
    )
    after_merge = plain_merge(after_first, merged_in, merge_weight)
    return plain_layer(devices, after_merge, second_routes, second_gates, second_gate_up, second_down)


def local(hidden_rows, *others):
    devices = lax.axis_size("inner")
    tok, width = hidden_rows.shape
    fits = 12 * devices * tok * width * 2 <= VMEM_LIMIT and devices % 4 == 0 and tok % 32 == 0
    return (fused if fits else unfused)(hidden_rows, *others)


def solution(mesh):
    rows = P(("groups", "inner"), None)
    return jax.shard_map(
        local,
        mesh=mesh,
        in_specs=(
            rows, rows, rows, rows,
            P("inner", None, None),
            P("inner", None, None),
            rows, rows,
            P("inner", None, None),
            P("inner", None, None),
            P(),
            P(),
            P("inner", None),
        ),
        out_specs=rows,
        check_vma=False,
    )
```
